32 devices in a mesh: dp: 8 (over y, x, core), tensor: 4 (over z).
Axes of the slice: x: 2, y: 2, z: 4, core: 2. Of those that a mesh axis runs over, the one named last changes fastest.
Arguments:
- inputs: float32 [8192, 1024], P('dp', 'tensor'), may hold values from -6 to 6
- norm_in: float32 [1024], replicated, may hold values from 0.5 to 1.5
- w_value: bfloat16 [1024, 2048], P(None, 'tensor'), may hold values from -0.1875 to 0.1875
- expand: float32 [1024, 16], P('tensor'), may hold values from -4 to 4
- ema_rate: float32 [1024, 16], P('tensor'), may hold values from 0.02 to 0.9
- damping: float32 [1024, 16], P('tensor'), may hold values from 0.3 to 1
- project: float32 [1024, 16], P('tensor'), may hold values from -1.5 to 1.5
- ema_skip: float32 [1024], P('tensor'), may hold values from -4 to 4
- w_shared: bfloat16 [1024, 128], P('tensor'), may hold values from -0.1875 to 0.1875
- qk_affine: float32 [3, 128], replicated, may hold values from -6 to 6
- w_reset: bfloat16 [1024, 2048], P('tensor'), may hold values from -0.1875 to 0.1875
- w_update: bfloat16 [1024, 1024], P('tensor'), may hold values from -0.1875 to 0.1875
- w_hidden: bfloat16 [1024, 1024], P('tensor'), may hold values from -0.1875 to 0.1875
- u_hidden: bfloat16 [2048, 1024], P('tensor'), may hold values from -0.375 to 0.375
- norm_out: float32 [1024], replicated, may hold values from 0.5 to 1.5
- w_in: bfloat16 [1024, 4096], P(None, 'tensor'), may hold values from -0.1875 to 0.1875
- w_out: bfloat16 [4096, 1024], P('tensor'), may hold values from -0.09375 to 0.09375
- cotangent: float32 [8192, 1024], P('dp', 'tensor'), may hold values from -6 to 6
- piece_starts: int32 [8, 2], P('dp'), may hold values from 0 to 768, as said below
Outputs:
- outputs: float32 [8192, 1024], P('dp', 'tensor')
- grad_inputs: float32 [8192, 1024], P('dp', 'tensor')
- grad_norm_in: float32 [1024], P('tensor')
- grad_w_value: float32 [1024, 2048], P('dp', 'tensor')
- grad_expand: float32 [1024, 16], P('tensor')
- grad_ema_rate: float32 [1024, 16], P('tensor')
- grad_damping: float32 [1024, 16], P('tensor')
- grad_project: float32 [1024, 16], P('tensor')
- grad_ema_skip: float32 [1024], P('tensor')
- grad_w_shared: float32 [1024, 128], P('tensor', 'dp')
- grad_qk_affine: float32 [3, 128], replicated
- grad_w_reset: float32 [1024, 2048], P('tensor', 'dp')
- grad_w_update: float32 [1024, 1024], P('tensor', 'dp')
- grad_w_hidden: float32 [1024, 1024], P('tensor', 'dp')
- grad_u_hidden: float32 [2048, 1024], P('tensor', 'dp')
- grad_norm_out: float32 [1024], P('tensor')
- grad_w_in: float32 [1024, 4096], P('dp', 'tensor')
- grad_w_out: float32 [4096, 1024], P('tensor', 'dp')
The draws below stay inside these ranges and needn't reach their ends.
Inputs may be any that keep to these rules, and one draw needn't show every extreme that they name: `piece_starts`: in each sequence the 2 picture pieces of 256 tokens start at these offsets, in rising order and without intersection; all other tokens are text. The first sequence's first piece starts at token 0 and the last sequence's last piece ends at the sequence's end.
All inputs are finite; a program needn't handle non-finite values.
Results may differ from the reference program's by a relative error of at most 0.018.
Values may be sent and summed in bfloat16 or wider, within the bound.
No kernel may reach another device: no remote copies, remote signals or barrier semaphores. Data moves between devices by JAX's collectives and lax.ppermute only.
A program may use at most 192 MiB of HBM per device.

```python
import math
import jax
import jax.numpy as jnp
from jax import lax

D = 1024
ZD = 128
VD = 2048
HD = 16
FF = 4096
LENGTH = 1024
PIECE = 256
PIECES = 2
QBLOCK = 512
EMA_BLOCK = 64
SEQS = 8
TOKENS = 8192


def draw_piece_starts(key, part):
    spare_room = LENGTH - PIECES * PIECE
    offsets = jax.random.randint(key, (SEQS, PIECES), 0, spare_room + 1)
    offsets = jnp.sort(offsets, axis=1)
    row_index = jnp.arange(SEQS, dtype=jnp.int32)[:, None]
    col_index = jnp.arange(PIECES, dtype=jnp.int32)[None, :]
    offsets = jnp.where((row_index == 0) & (col_index == 0), 0, offsets)
    offsets = jnp.where((row_index == SEQS - 1) & (col_index == PIECES - 1), spare_room, offsets)
    return (offsets + PIECE * jnp.arange(PIECES, dtype=jnp.int32)[None, :]).astype(jnp.int32)


def shard_levels(stream_key, extent, shards, smallest, high):
    def one(dim, shards_of):
        heights = jax.random.uniform(jax.random.fold_in(jax.random.fold_in(stream_key, 6), dim), (shards_of,), jnp.float32, smallest / len(shards), high / len(shards))
        return jnp.repeat(jnp.exp(heights), extent[dim] // shards_of).reshape((-1,) + (1,) * (len(extent) - dim - 1))

    factor_of = one(*shards[0])
    for cut in shards[1:]:
        factor_of = factor_of * one(*cut)
    return factor_of


def noise(key, extent, spread, reach, cuts=(), held_as=jnp.bfloat16):
    array = jax.random.normal(key, extent, jnp.float32) * spread
    if len(cuts) > 0:
        array = shard_levels(key, extent, cuts, -0.22, 0.18) * array
    return jnp.clip(array, min=-reach, max=reach).astype(held_as)


def setup_inputs(seed: int = 0) -> dict:
    streams_of = jax.random.split(jax.random.key(seed), 20)
    return {
        "inputs": noise(streams_of[0], (TOKENS, D), 1.0, 6.0, ((0, 8), (1, 4)), jnp.float32),
        "norm_in": jnp.clip(1.0 + 0.1 * jax.random.normal(streams_of[1], (D,), jnp.float32), 0.5, 1.5),
        "w_value": noise(streams_of[2], (D, VD), D ** -0.5, 0.1875, ((1, 4),)),
        "expand": noise(streams_of[3], (D, HD), 1.0, 4.0, ((0, 4),), jnp.float32),
        "ema_rate": jnp.clip(jnp.exp(math.log(0.9) - 3.8066625 * jax.random.uniform(streams_of[4], (D, HD), jnp.float32) ** shard_levels(streams_of[4], (D, HD), ((0, 4),), -0.2, 0.2)), 0.02, 0.9),
        "damping": jnp.clip(0.3 + 0.7 * jax.random.uniform(streams_of[5], (D, HD), jnp.float32) ** shard_levels(streams_of[5], (D, HD), ((0, 4),), -0.2, 0.2), 0.3, 1.0),
        "project": noise(streams_of[6], (D, HD), HD ** -0.5, 1.5, ((0, 4),), jnp.float32),
        "ema_skip": noise(streams_of[7], (D,), 1.0, 4.0, ((0, 4),), jnp.float32),
        "w_shared": noise(streams_of[8], (D, ZD), D ** -0.5, 0.1875, ((0, 4),)),
        "qk_affine": noise(streams_of[9], (3, ZD), 1.5, 6.0, (), jnp.float32),
        "w_reset": noise(streams_of[10], (D, VD), D ** -0.5, 0.1875, ((0, 4),)),
        "w_update": noise(streams_of[11], (D, D), D ** -0.5, 0.1875, ((0, 4),)),
        "w_hidden": noise(streams_of[12], (D, D), D ** -0.5, 0.1875, ((0, 4),)),
        "u_hidden": noise(streams_of[13], (VD, D), (VD // 8) ** -0.5, 0.375, ((0, 4),)),
        "norm_out": jnp.clip(1.0 + 0.1 * jax.random.normal(streams_of[14], (D,), jnp.float32), 0.5, 1.5),
        "w_in": noise(streams_of[15], (D, FF), D ** -0.5, 0.1875, ((1, 4),)),
        "w_out": noise(streams_of[16], (FF, D), FF ** -0.5, 0.09375, ((0, 4),)),
        "cotangent": noise(streams_of[17], (TOKENS, D), 1.0, 6.0, ((0, 8), (1, 4)), jnp.float32),
        "piece_starts": draw_piece_starts(jax.random.fold_in(streams_of[19], 71), 0),
    }


epsilon = 1e-05
highest = lax.Precision.HIGHEST

@jax.custom_vjp
def low(v):
    return lax.optimization_barrier(v.astype(jnp.bfloat16)).astype(jnp.float32)

@jax.custom_vjp
def low_back(v):
    return v

def low_keep(v):
    return (low(v), None)

def low_pass(kept, grad):
    return (grad,)

def back_keep(v):
    return (v, None)

def back_low(kept, grad):
    return (low(grad),)
low.defvjp(low_keep, low_pass)
low_back.defvjp(back_keep, back_low)

def matmul(left, right):
    return jnp.dot(left, right, precision=highest, preferred_element_type=jnp.float32)

def normalize(values):
    centered = values - lax.optimization_barrier(jnp.mean(values, axis=-1, keepdims=True))
    return centered * lax.rsqrt(lax.optimization_barrier(jnp.mean(centered * centered, axis=-1, keepdims=True)) + epsilon)

def toeplitz_table(kernel):
    block_size = kernel.shape[0]
    rows = jnp.arange(block_size, dtype=jnp.int32)
    lag = rows[:, None] - rows[None, :]
    picked = jnp.take(kernel, jnp.maximum(lag, 0), axis=0)
    return jnp.where((lag >= 0)[:, :, None], picked, jnp.zeros_like(picked))

def ema_mix(signal, expand, ema_rate, damping, project, ema_skip):
    length = signal.shape[0]
    channels = signal.shape[1]
    block_size = EMA_BLOCK
    decays = 1.0 - ema_rate * damping
    log_decay = jnp.log(decays)
    step_index = jnp.arange(block_size).astype(jnp.float32)
    powers = jnp.exp(step_index[:, None, None] * log_decay[None, :, :])
    inject = ema_rate * expand
    kernel = lax.optimization_barrier(jnp.sum(powers * (project * inject)[None, :, :], axis=2))
    toeplitz = toeplitz_table(kernel)
    blocks = signal.reshape(length // block_size, block_size, channels)
    in_block = jnp.einsum('ijc,njc->nic', toeplitz, blocks, precision=highest)
    driving = jnp.einsum('jch,njc->nch', powers[::-1] * inject[None, :, :], blocks, precision=highest)
    block_decay = jnp.exp(block_size * log_decay)

    def advance(carried, pushed):
        return (block_decay * carried + pushed, carried)
    unused, before = lax.scan(advance, jnp.zeros_like(decays), driving)
    from_before = jnp.einsum('ich,nch->nic', powers * (decays * project)[None, :, :], before, precision=highest)
    mixed_sum = (in_block + from_before).reshape(length, channels)
    return jax.nn.silu(mixed_sum + ema_skip * signal)

def piece_ids_of(starts, length):
    positions = jnp.arange(length, dtype=jnp.int32)
    inside = (positions[:, None] >= starts[None, :]) & (positions[:, None] < starts[None, :] + PIECE)
    labels = jnp.arange(1, starts.shape[0] + 1, dtype=jnp.int32)
    return lax.optimization_barrier(jnp.sum(jnp.where(inside, labels[None, :], 0), axis=1)).astype(jnp.int32)

def allowed_keys(row_pos, row_ids, piece_ids):
    key_pos = jnp.arange(piece_ids.shape[0], dtype=jnp.int32)
    causal = key_pos[None, :] <= row_pos[:, None]
    same_piece = (row_ids[:, None] == piece_ids[None, :]) & (row_ids[:, None] > 0)
    return causal | same_piece

def attend(queries, keys_low, values, piece_ids):
    length = queries.shape[0]
    score_scale = queries.shape[1] ** (-0.5)

    def one_block(block_index):
        first_row = block_index * QBLOCK
        query_rows = lax.dynamic_slice_in_dim(queries, first_row, QBLOCK, 0)
        row_pos = first_row + jnp.arange(QBLOCK, dtype=jnp.int32)
        row_ids = lax.dynamic_slice_in_dim(piece_ids, first_row, QBLOCK, 0)
        scores = matmul(query_rows, keys_low.T) * score_scale
        scores = jnp.where(allowed_keys(row_pos, row_ids, piece_ids), scores, -1e+30)
        weights = jax.nn.softmax(scores, axis=-1)
        return matmul(low(weights), values)
    blocks = lax.map(jax.checkpoint(one_block), jnp.arange(length // QBLOCK, dtype=jnp.int32))
    return blocks.reshape(length, values.shape[1])

def mega_layer(seq_in, weights, piece_ids):
    norm_in, w_value, expand, ema_rate, damping, project, ema_skip, w_shared, qk_affine, w_reset, w_update, w_hidden, u_hidden, norm_out, w_in, w_out = weights
    normed = normalize(seq_in) * norm_in
    normed_low = low(normed)
    values_low = low(jax.nn.silu(low_back(matmul(normed_low, w_value))))
    mixer_low = low(ema_mix(normed, expand, ema_rate, damping, project, ema_skip))
    shared = jax.nn.silu(low_back(matmul(mixer_low, w_shared)))
    queries = low(shared * qk_affine[0] + qk_affine[1])
    keys_low = low(shared * qk_affine[2])
    attended = low_back(attend(queries, keys_low, values_low, piece_ids))
    reset_gate = jax.nn.silu(low_back(matmul(mixer_low, w_reset)))
    update = jax.nn.sigmoid(low_back(matmul(mixer_low, w_update)))
    gated_low = low(reset_gate * attended)
    candidate = jax.nn.silu(low_back(matmul(mixer_low, w_hidden) + matmul(gated_low, u_hidden)))
    new_state = update * candidate + (1.0 - update) * seq_in
    state_low = low(normalize(new_state) * norm_out)
    ffn_low = low(jax.nn.silu(low_back(matmul(state_low, w_in))))
    return new_state + low_back(matmul(ffn_low, w_out))

def reference(inputs, norm_in, w_value, expand, ema_rate, damping, project, ema_skip, w_shared, qk_affine, w_reset, w_update, w_hidden, u_hidden, norm_out, w_in, w_out, cotangent, piece_starts):
    params = (norm_in.astype(jnp.float32), w_value.astype(jnp.float32), expand.astype(jnp.float32), ema_rate.astype(jnp.float32), damping.astype(jnp.float32), project.astype(jnp.float32), ema_skip.astype(jnp.float32), w_shared.astype(jnp.float32), qk_affine.astype(jnp.float32), w_reset.astype(jnp.float32), w_update.astype(jnp.float32), w_hidden.astype(jnp.float32), u_hidden.astype(jnp.float32), norm_out.astype(jnp.float32), w_in.astype(jnp.float32), w_out.astype(jnp.float32))
    sequences = inputs.astype(jnp.float32).reshape(SEQS, LENGTH, D)
    cotangents = cotangent.astype(jnp.float32).reshape(SEQS, LENGTH, D)

    def one_sequence(totals, sequence_item):
        seq_in, seq_grad, starts = sequence_item
        piece_ids = piece_ids_of(starts, LENGTH)

        def forward(layer_in, layer_params):
            return mega_layer(layer_in, layer_params, piece_ids)
        result, pull = jax.vjp(forward, seq_in, params)
        input_grad, param_grads = pull(seq_grad)
        return (jax.tree.map(jnp.add, totals, param_grads), (result, input_grad))
    zeros_start = jax.tree.map(jnp.zeros_like, params)
    totals, (results, input_grads) = lax.scan(one_sequence, zeros_start, (sequences, cotangents, piece_starts))
    return (results.reshape(TOKENS, D), input_grads.reshape(TOKENS, D), totals[0], totals[1], totals[2], totals[3], totals[4], totals[5], totals[6], totals[7], totals[8], totals[9], totals[10], totals[11], totals[12], totals[13], totals[14], totals[15])
```

```python
import jax
import jax.numpy as jnp
import numpy as np
from jax import lax
from jax.experimental import pallas as pl
from jax.experimental.pallas import tpu as pltpu
from jax.sharding import Mesh, PartitionSpec as P

f32 = jnp.float32
bf16 = jnp.bfloat16
PIECE = 256
EPS = 1e-5
HD = 16
CH = 8
LT = 128

GROUP = ("xx", "core", "tensor")
PLANE = ("yy", "xx")
DPS = ("yy", "xx", "rest", "core")
ALL = DPS + ("tensor",)

VM = pl.BlockSpec(memory_space=pltpu.VMEM)
SM = pl.BlockSpec(memory_space=pltpu.SMEM)


def shape(dims, dtype):
    return jax.ShapeDtypeStruct(tuple(dims), dtype)


def call(body, outs, idx, *args, name, scratch=(), flops=0, limit=48):
    return pl.pallas_call(
        body,
        out_shape=tuple(outs),
        in_specs=[SM] + [VM] * len(args),
        out_specs=(VM,) * len(outs),
        scratch_shapes=list(scratch),
        name=name,
        compiler_params=pltpu.CompilerParams(vmem_limit_bytes=limit << 20),
    )(idx, *args)


def dot(a, b):
    return jnp.dot(a, b, preferred_element_type=f32)


def dot_t(a, b):
    return lax.dot_general(a, b, (((1,), (1,)), ((), ())), preferred_element_type=f32)


def t_dot(a, b):
    return lax.dot_general(a, b, (((0,), (0,)), ((), ())), preferred_element_type=f32)


def sig(v):
    return 1.0 / (1.0 + jnp.exp(-v))


def silu(v):
    return v * sig(v)


def silu_grad(v):
    s = sig(v)
    return s * (1.0 + v * (1.0 - s))


def at(i, n):
    return pl.ds(pl.multiple_of(i * n, n), n)


def _params(par_ref, lanes):
    expand = par_ref[0:16, lanes]; rate = par_ref[16:32, lanes]
    damp = par_ref[32:48, lanes]; proj = par_ref[48:64, lanes]
    dec = 1.0 - rate*damp
    coef = proj*rate*expand
    return expand, rate, damp, proj, dec, coef

def _rows(a):
    return [jnp.broadcast_to(a[h:h+1], (CH, LT)) for h in range(HD)]

def _pow(a, n):
    out=None; base=a
    while n:
        if n&1: out = base if out is None else out*base
        n >>= 1
        if n: base = base*base
    return out

def _carry_down(s, decl):
    row = lax.broadcasted_iota(jnp.int32, (CH, LT), 0)
    out=[]
    for h in range(HD):
        v = s[h]; p = decl[h]
        for d in (1,2,4):
            v = v + p*jnp.where(row >= d, pltpu.roll(v, d, 0), 0.0)
            p = p*p
        out.append(jnp.where(row >= 1, pltpu.roll(v, 1, 0), 0.0))
    return out

def _carry_up(s, decl):
    row = lax.broadcasted_iota(jnp.int32, (CH, LT), 0)
    out=[]
    for h in range(HD):
        v = s[h]; p = decl[h]
        for d in (1,2,4):
            v = v + p*jnp.where(row < CH-d, pltpu.roll(v, CH-d, 0), 0.0)
            p = p*p
        out.append(jnp.where(row < CH-1, pltpu.roll(v, CH-1, 0), 0.0))
    return out

def fwd_kernel(x_ref, par_ref, skip_ref, m_ref, low_ref, s0_ref, xs, ms):
    T, W = x_ref.shape
    L = T//CH
    for lt in range(W//LT):
        lanes = slice(lt*LT, (lt+1)*LT)
        *_, dec, coef = _params(par_ref, lanes)
        dec = _rows(dec); coef=_rows(coef)
        skip = jnp.broadcast_to(skip_ref[0:1, lanes], (CH, LT))
        z = jnp.zeros((CH,LT), f32)
        xs[...] = x_ref[:, lanes]
        def one(i, s):
            xi = xs[pl.ds(i, CH, stride=L), :]
            return tuple(dec[h]*s[h]+xi for h in range(HD))
        s = lax.fori_loop(0, L, one, (z,)*HD, unroll=8)
        s0 = _carry_down(s, [_pow(dec[h], L) for h in range(HD)])
        for h in range(HD):
            s0_ref[h, :, lanes] = s0[h]
        def two(i, s):
            xi = xs[pl.ds(i, CH, stride=L), :]
            s = tuple(dec[h]*s[h]+xi for h in range(HD))
            y = skip*xi
            terms=[coef[h]*s[h] for h in range(HD)]
            while len(terms)>1:
                terms=[terms[k]+terms[k+1] for k in range(0,len(terms),2)]
            ms[pl.ds(i, CH, stride=L), :] = y+terms[0]
            return s
        lax.fori_loop(0, L, two, tuple(s0), unroll=4)
        m_ref[:, lanes] = ms[...]
        low_ref[:, lanes] = silu(ms[...]).astype(bf16)

def bwd_kernel(g_ref, m_ref, x_ref, par_ref, skip_ref, s0_ref, eg_ref, gp_ref, gm_ref, st_ref, xs, gs_ref, es):
    T, W = x_ref.shape
    L = T//CH
    for lt in range(W//LT):
        lanes = slice(lt*LT, (lt+1)*LT)
        expand, rate, damp, proj, dec2, coef2 = _params(par_ref, lanes)
        dec=_rows(dec2); coef=_rows(coef2)
        skip = jnp.broadcast_to(skip_ref[0:1, lanes], (CH, LT))
        z = jnp.zeros((CH,LT), f32)
        xs[...] = x_ref[:, lanes]
        m = m_ref[:, lanes]
        sg = 1.0/(1.0+jnp.exp(-m))
        gs_ref[...] = g_ref[:, lanes].astype(f32)*(sg*(1.0+m*(1.0-sg)))
        def one(k, c):
            b, gs = c
            i = L-1-k
            gm = gs_ref[pl.ds(i, CH, stride=L), :]
            gm_ref[i] = gm
            xi = xs[pl.ds(i, CH, stride=L), :]
            gs = gs + gm*xi
            return (tuple(dec[h]*b[h]+gm for h in range(HD)), gs)
        b, gs = lax.fori_loop(0, L, one, ((z,)*HD, z), unroll=4)
        e = _carry_up(b, [_pow(dec[h], L) for h in range(HD)])
        s0 = [s0_ref[h, :, lanes] for h in range(HD)]
        for h in range(HD): st_ref[0, h] = s0[h]
        def rec(i, s):
            xi = xs[pl.ds(i, CH, stride=L), :]
            s = tuple(dec[h]*s[h]+xi for h in range(HD))
            for h in range(HD): st_ref[i+1, h] = s[h]
            return s
        lax.fori_loop(0, L, rec, tuple(s0), unroll=4)
        gcoef=[]; gdec=[]
        G=8
        for g0 in range(0, HD, G):
            hs = range(g0, g0+G)
            def two(k, c):
                b, gc, gd = c
                i = L-1-k
                gm = gm_ref[i]
                b = tuple(dec[h]*b[j]+gm for j,h in enumerate(hs))
                gc = tuple(gc[j]+gm*st_ref[i+1,h] for j,h in enumerate(hs))
                gd = tuple(gd[j]+b[j]*st_ref[i,h] for j,h in enumerate(hs))
                terms=[coef[h]*b[j] for j,h in enumerate(hs)]
                while len(terms)>1:
                    terms=[terms[q]+terms[q+1] for q in range(0,len(terms),2)]
                if g0==0: base = skip*gm
                else: base = es[pl.ds(i, CH, stride=L), :]
                es[pl.ds(i, CH, stride=L), :] = base+terms[0]
                return (b, gc, gd)
            zz=(z,)*G
            _, gc, gd = lax.fori_loop(0, L, two, (tuple(e[h] for h in hs), zz, zz), unroll=2)
            gcoef += list(gc); gdec += list(gd)
        eg_ref[:, lanes] = es[...]
        gcoef = jnp.concatenate([jnp.sum(v,0,keepdims=True) for v in gcoef],0)
        gdec = jnp.concatenate([jnp.sum(v,0,keepdims=True) for v in gdec],0)*coef2
        gp_ref[0:16, lanes] = gcoef*proj*rate
        gp_ref[16:32, lanes] = gcoef*proj*expand - gdec*damp
        gp_ref[32:48, lanes] = -gdec*rate
        gp_ref[48:64, lanes] = gcoef*rate*expand
        gp_ref[64:72, lanes] = jnp.broadcast_to(jnp.sum(gs,0,keepdims=True),(8,LT))

def ema_fwd(x, par, skip):
    T,W = x.shape
    return pl.pallas_call(fwd_kernel, out_shape=(jax.ShapeDtypeStruct((T,W),f32), jax.ShapeDtypeStruct((T,W),bf16), jax.ShapeDtypeStruct((HD,CH,W),f32)),
        in_specs=[VM]*3, out_specs=(VM,VM,VM), name="ema_fwd", scratch_shapes=[pltpu.VMEM((T,LT),f32)]*2,
        compiler_params=pltpu.CompilerParams(vmem_limit_bytes=48<<20))(x,par,skip)
def ema_bwd(g,m,x,par,skip,s0):
    T,W = x.shape
    return pl.pallas_call(bwd_kernel, out_shape=(jax.ShapeDtypeStruct((T,W),f32), jax.ShapeDtypeStruct((72,W),f32)),
        in_specs=[VM]*6, out_specs=(VM,VM), name="ema_bwd",
        scratch_shapes=[pltpu.VMEM((T//CH,CH,LT),f32), pltpu.VMEM((T//CH+1,HD,CH,LT),f32)]+[pltpu.VMEM((T,LT),f32)]*3,
        compiler_params=pltpu.CompilerParams(vmem_limit_bytes=48<<20))(g,m,x,par,skip,s0)


def tile(loc, rem, q, rel, s):
    return loc[q ^ rel] if s == 0 else rem[rel][s - 1]


def value_kernel(idx, n0, n1, o0, o1, loc, r0, r1, r2, r3, full, pre, val):
    z, q, c, x = idx[0], idx[1], idx[2], idx[3]
    rem = (r0, r1, r2, r3)
    full[:, at(2 * c + x, 256)] = n0[...]
    full[:, at(2 * c + 1 - x, 256)] = n1[...]
    full[:, at(2 - 2 * c + x, 256)] = o0[...]
    full[:, at(3 - 2 * c - x, 256)] = o1[...]
    for s in range(4):
        acc = None
        for rel in range(4):
            t = dot(full[:, at(q ^ rel, 256)], tile(loc, rem, q, rel, s))
            acc = t if acc is None else acc + t
        v = at(lax.rem(z + 4 - s, 4), 256)
        pre[:, v] = acc
        val[:, v] = silu(acc).astype(bf16)


def proj_kernel(
    idx, n0, n1, o0, o1, loc, r0, r1, r2, r3, wsl, ws1, ws2, ws3, aff,
    full, reset, update, hidden, shp, qs, ks,
):
    z, q, c, x = idx[0], idx[1], idx[2], idx[3]
    rem = (r0, r1, r2, r3)
    full[:, at(2 * c + x, 256)] = n0[...]
    full[:, at(2 * c + 1 - x, 256)] = n1[...]
    full[:, at(2 - 2 * c + x, 256)] = o0[...]
    full[:, at(3 - 2 * c - x, 256)] = o1[...]
    rows = [full[:, at(lax.rem(z + 4 - s, 4), 256)] for s in range(4)]
    acc = None
    for s, w in enumerate((wsl, ws1, ws2, ws3)):
        t = dot(rows[s], w[...])
        acc = t if acc is None else acc + t
    shp[...] = acc
    sh = silu(acc)
    qs[...] = (sh * aff[0:1, :] + aff[1:2, :]).astype(bf16)
    ks[...] = (sh * aff[2:3, :]).astype(bf16)
    for rel in range(4):
        acc = None
        for s in range(4):
            t = dot(rows[s], tile(loc, rem, q, rel, s))
            acc = t if acc is None else acc + t
        b = q ^ rel
        reset[:, at(b, 256)] = acc[:, 0:256]
        update[:, at(b, 128)] = acc[:, 256:384]
        hidden[:, at(b, 128)] = acc[:, 384:512]


def attend_kernel(
    idx, qs, ko, kn, vo, vn, reset, loc, r0, r1, r2, r3, probs, att, gated, own, send, part,
):
    z, q, c, x = idx[0], idx[1], idx[2], idx[3]
    rem = (r0, r1, r2, r3)
    t = qs.shape[0]
    scale = qs.shape[1] ** (-0.5)
    tm = 256
    for i in range(t // tm):
        r = slice(i * tm, (i + 1) * tm)
        row = x * t + i * tm + lax.broadcasted_iota(jnp.int32, (tm, t), 0)
        parts = []
        for k, half in ((ko, x), (kn, 1 - x)):
            col = half * t + lax.broadcasted_iota(jnp.int32, (tm, t), 1)
            seen = col <= row
            for n in range(2):
                first = idx[4 + n]
                lo = jnp.minimum(row, col) >= first
                hi = jnp.maximum(row, col) < first + PIECE
                seen = seen | (lo & hi)
            parts.append(jnp.where(seen, dot_t(qs[r, :], k[...]) * scale, -1e30))
        top = jnp.maximum(
            jnp.max(parts[0], axis=1, keepdims=True), jnp.max(parts[1], axis=1, keepdims=True)
        )
        e = [jnp.exp(p - top) for p in parts]
        total = jnp.sum(e[0], axis=1, keepdims=True) + jnp.sum(e[1], axis=1, keepdims=True)
        inv = 1.0 / total
        p = [(v * inv).astype(bf16) for v in e]
        probs[r, 0:t] = p[0]
        probs[r, t : 2 * t] = p[1]
        a = dot(p[0], vo[...]) + dot(p[1], vn[...])
        att[r, :] = a
        gated[r, :] = (silu(reset[r, :]) * a).astype(bf16)
    for rel in range(4):
        acc = None
        for s in range(4):
            v = dot(gated[:, at(lax.rem(z + 4 - s, 4), 256)], tile(loc, rem, q, rel, s))
            acc = v if acc is None else acc + v
        part[:, at(q ^ rel, 256)] = acc
    own[...] = part[:, at(c, 512)]
    send[...] = part[:, at(1 - c, 512)].astype(bf16)


def state_kernel(idx, hidden, own, recv, upd, xs, hpre, state, st):
    h = hidden[...] + own[...] + recv[...].astype(f32)
    hpre[...] = h
    u = sig(upd[...])
    v = u * silu(h) + (1.0 - u) * xs[...]
    state[...] = v
    mean = jnp.mean(v, axis=1, keepdims=True)
    second = jnp.sum(jnp.square(v - mean), axis=1, keepdims=True)
    lane = lax.broadcasted_iota(jnp.int32, st.shape, 1)
    st[...] = jnp.where(lane < 64, mean, second)


def unit_of(state, st, so):
    w = state.shape[1]
    m0, m1 = st[:, 0:1], so[:, 0:1]
    mean = 0.5 * (m0 + m1)
    total = st[:, 64:65] + so[:, 64:65] + w * (jnp.square(m0 - mean) + jnp.square(m1 - mean))
    inv = lax.rsqrt(total / (2 * w) + EPS)
    return (state[...] - mean) * inv, inv


def unit_kernel(idx, state, st, so, gain, low):
    unit, _ = unit_of(state, st, so)
    low[...] = (unit * gain[...]).astype(bf16)


def join(full, a, b, c):
    w = a.shape[1]
    full[:, at(c, w)] = a[...]
    full[:, at(1 - c, w)] = b[...]


def ffn_kernel(
    idx, s0, s1, g0, g1, il, i0, i1, i2, i3, ol, o0, o1, o2, o3,
    sf, gf, low, gffn, own, send, part,
):
    q, c = idx[1], idx[2]
    ri, ro = (i0, i1, i2, i3), (o0, o1, o2, o3)
    join(sf, s0, s1, c)
    join(gf, g0, g1, c)
    for s in range(4):
        f = slice(s * 512, (s + 1) * 512)
        pre = None
        for rel in range(4):
            t = dot(sf[:, at(q ^ rel, 256)], tile(il, ri, q, rel, s))
            pre = t if pre is None else pre + t
        low[:, f] = silu(pre).astype(bf16)
        g = None
        for rel in range(4):
            t = dot_t(gf[:, at(q ^ rel, 256)], tile(ol, ro, q, rel, s))
            g = t if g is None else g + t
        gffn[:, f] = (g * silu_grad(pre)).astype(bf16)
    for rel in range(4):
        acc = None
        for s in range(4):
            t = dot_t(gffn[:, s * 512 : (s + 1) * 512], tile(il, ri, q, rel, s))
            acc = t if acc is None else acc + t
        part[:, at(q ^ rel, 256)] = acc
    own[...] = part[:, at(c, 512)]
    send[...] = part[:, at(1 - c, 512)].astype(bf16)


def branch_kernel(idx, low, ol, o0, o1, o2, o3, own, send, part):
    q, c = idx[1], idx[2]
    ro = (o0, o1, o2, o3)
    for rel in range(4):
        acc = None
        for s in range(4):
            t = dot(low[:, s * 512 : (s + 1) * 512], tile(ol, ro, q, rel, s))
            acc = t if acc is None else acc + t
        part[:, at(q ^ rel, 256)] = acc
    own[...] = part[:, at(c, 512)]
    send[...] = part[:, at(1 - c, 512)].astype(bf16)


def grad_out_kernel(idx, low, gf, *outs):
    q = idx[1]
    n = outs[0].shape[1]
    for s in range(4):
        a = low[:, s * n : (s + 1) * n]
        for rel in range(4):
            outs[rel][s] = t_dot(a, gf[:, at(q ^ rel, 256)]).astype(bf16)


def grad_in_kernel(idx, sf, gffn, *outs):
    q = idx[1]
    n = outs[0].shape[2]
    for rel in range(4):
        a = sf[:, at(q ^ rel, 256)]
        for s in range(4):
            outs[rel][s] = t_dot(a, gffn[:, s * n : (s + 1) * n]).astype(bf16)


def grad_unit_kernel(idx, own, recv, state, st, so, gain, gu, st2, gno):
    unit, _ = unit_of(state, st, so)
    g = own[...] + recv[...].astype(f32)
    gu[...] = g
    gno[...] = jnp.sum(g * unit, axis=0, keepdims=True)
    gn = g * gain[...]
    lane = lax.broadcasted_iota(jnp.int32, st2.shape, 1)
    st2[...] = jnp.where(
        lane < 64, jnp.sum(gn, axis=1, keepdims=True), jnp.sum(gn * unit, axis=1, keepdims=True)
    )


def grad_state_kernel(idx, gu, state, st, so, t0, t1, gain, cot, hpre, upd, xs, ug, hg, gi):
    unit, inv = unit_of(state, st, so)
    d = 2 * state.shape[1]
    m1 = (t0[:, 0:1] + t1[:, 0:1]) / d
    m2 = (t0[:, 64:65] + t1[:, 64:65]) / d
    gs = cot[...] + inv * (gu[...] * gain[...] - m1 - unit * m2)
    u = sig(upd[...])
    h = hpre[...]
    s = sig(h)
    ug[...] = (gs * (h * s - xs[...]) * u * (1.0 - u)).astype(bf16)
    hg[...] = (gs * u * (s * (1.0 + h * (1.0 - s)))).astype(bf16)
    gi[...] = gs * (1.0 - u)


def gate_kernel(
    idx, h0, h1, ug, reset, att, probs, loc, r0, r1, r2, r3, hf, cat, gatt, vsend, gr,
):
    z, q, c = idx[0], idx[1], idx[2]
    rem = (r0, r1, r2, r3)
    t = h0.shape[0]
    join(hf, h0, h1, c)
    for s in range(4):
        v = at(lax.rem(z + 4 - s, 4), 256)
        g = None
        for rel in range(4):
            w = dot_t(hf[:, at(q ^ rel, 256)], tile(loc, rem, q, rel, s))
            g = w if g is None else g + w
        r = reset[:, v]
        sg = sig(r)
        gatt[:, v] = (g * (r * sg)).astype(bf16)
        gr[:, v] = (g * att[:, v] * (sg * (1.0 + r * (1.0 - sg)))).astype(bf16)
    for rel in range(4):
        b = q ^ rel
        cat[rel, :, 0:256] = gr[:, at(b, 256)]
        cat[rel, :, 256:384] = ug[:, at(b, 128)]
        cat[rel, :, 384:512] = h0[:, at(b, 128)]
    vsend[...] = t_dot(probs[:, t : 2 * t], gatt[...]).astype(bf16)


def attend_back_kernel(idx, probs, gatt, vo, vn, ko, kn, qs, qg, kown, ksend, vown):
    t = qs.shape[0]
    scale = qs.shape[1] ** (-0.5)
    p = [probs[:, 0:t].astype(f32), probs[:, t : 2 * t].astype(f32)]
    g = [dot_t(gatt[...], vo[...]), dot_t(gatt[...], vn[...])]
    center = jnp.sum(p[0] * g[0], axis=1, keepdims=True) + jnp.sum(p[1] * g[1], axis=1, keepdims=True)
    gs = [(a * (b - center) * scale).astype(bf16) for a, b in zip(p, g)]
    ksend[...] = t_dot(gs[1], qs[...]).astype(bf16)
    qg[...] = dot(gs[0], ko[...]) + dot(gs[1], kn[...])
    kown[...] = t_dot(gs[0], qs[...])
    vown[...] = t_dot(probs[:, 0:t], gatt[...])


def value_back_kernel(idx, vown, vrecv, pre, loc, r0, r1, r2, r3, gv, own, send, part):
    z, q, c = idx[0], idx[1], idx[2]
    rem = (r0, r1, r2, r3)
    gv[...] = ((vown[...] + vrecv[...].astype(f32)) * silu_grad(pre[...])).astype(bf16)
    for rel in range(4):
        acc = None
        for s in range(4):
            w = dot_t(gv[:, at(lax.rem(z + 4 - s, 4), 256)], tile(loc, rem, q, rel, s))
            acc = w if acc is None else acc + w
        part[:, at(q ^ rel, 256)] = acc
    own[...] = part[:, at(c, 512)]
    send[...] = part[:, at(1 - c, 512)].astype(bf16)


def mixer_back_kernel(
    idx, cat, loc, r0, r1, r2, r3, wsl, ws1, ws2, ws3, aff, shp, qg, kown, krecv, gs, ga, own, send, part,
):
    z, q, c = idx[0], idx[1], idx[2]
    rem = (r0, r1, r2, r3)
    kg = kown[...] + krecv[...].astype(f32)
    s_pre = shp[...]
    sh = silu(s_pre)
    g = qg[...]
    gs[...] = ((g * aff[0:1, :] + kg * aff[2:3, :]) * silu_grad(s_pre)).astype(bf16)
    ga[0:1, :] = jnp.sum(g * sh, axis=0, keepdims=True)
    ga[1:2, :] = jnp.sum(g, axis=0, keepdims=True)
    ga[2:3, :] = jnp.sum(kg * sh, axis=0, keepdims=True)
    for s, w in enumerate((wsl, ws1, ws2, ws3)):
        acc = dot_t(gs[...], w[...])
        for rel in range(4):
            acc = acc + dot_t(cat[rel], tile(loc, rem, q, rel, s))
        part[:, at(lax.rem(z + 4 - s, 4), 256)] = acc
    own[...] = part[:, at(c, 512)]
    send[...] = part[:, at(1 - c, 512)].astype(bf16)


def grad_pack_kernel(idx, mf, cat, *outs):
    z = idx[0]
    for s in range(4):
        a = mf[:, at(lax.rem(z + 4 - s, 4), 256)]
        for rel in range(4):
            outs[rel][s] = t_dot(a, cat[rel]).astype(bf16)


def grad_u_kernel(idx, gated, hf, *outs):
    z, q = idx[0], idx[1]
    for s in range(4):
        a = gated[:, at(lax.rem(z + 4 - s, 4), 256)]
        for rel in range(4):
            outs[rel][s] = t_dot(a, hf[:, at(q ^ rel, 256)]).astype(bf16)


def grad_value_kernel(idx, nf, gv, mf, gs, o0, o1, o2, o3, gws):
    z, q = idx[0], idx[1]
    outs = (o0, o1, o2, o3)
    for rel in range(4):
        a = nf[:, at(q ^ rel, 256)]
        for s in range(4):
            outs[rel][s] = t_dot(a, gv[:, at(lax.rem(z + 4 - s, 4), 256)]).astype(bf16)
    gws[...] = t_dot(mf[...], gs[...])


def place(k):
    return [
        ((x * 2 + c) * 4 + z, (((z + k) % 2) * 2 + z // 2) * 4 + 2 * x + c)
        for x in range(2)
        for c in range(2)
        for z in range(4)
    ]


def pick(pred, a, b, axis):
    return jnp.where(pred, jnp.concatenate([a, b], axis), jnp.concatenate([b, a], axis))


def to_chips(a):
    z = lax.axis_index("tensor")
    halves = a.reshape(2, a.shape[0] // 2, a.shape[1])
    return [
        lax.ppermute(lax.dynamic_index_in_dim(halves, (z + k) % 2, 0, False), GROUP, place(k))
        for k in range(2)
    ]


def from_chips(a):
    z = lax.axis_index("tensor")
    x = lax.axis_index("xx")
    w = a.shape[1] // 2
    r = [
        lax.ppermute(
            lax.dynamic_slice_in_dim(a, ((x + k) % 2) * w, w, 1),
            GROUP,
            [(t, s) for s, t in place(k)],
        )
        for k in range(2)
    ]
    return pick(z % 2 == 0, r[0], r[1], 0)


def swap2(a, axis):
    return lax.ppermute(a, axis, [(0, 1), (1, 0)])


def shifted(a, axis, count, s):
    return lax.ppermute(a, axis, [(i, (i + s) % count) for i in range(count)])


def moments(rows, axis, count):
    width = rows.shape[1]
    mean = jnp.mean(rows, axis=1)
    second = jnp.sum(jnp.square(rows - mean[:, None]), axis=1)
    both = jnp.stack([mean, second])
    parts = [both] + [shifted(both, axis, count, s) for s in range(1, count)]
    total_mean = sum(p[0] for p in parts) / count
    total = sum(p[1] + width * jnp.square(p[0] - total_mean) for p in parts)
    return total_mean[:, None], lax.rsqrt(total / (width * count) + EPS)[:, None]


def sum_over(v, axis, count):
    return v + sum(shifted(v, axis, count, s) for s in range(1, count))


def sum_devices(v, rest, axes):
    for a in axes:
        v = v + (swap2(v, a) if a != "tensor" else sum(shifted(v, a, 4, s) for s in range(1, 4)))
    return lax.psum(v, "rest") if rest > 1 else v


def gather(loc, q, x_first):
    mine = lax.dynamic_index_in_dim(loc, q, 0, False)
    three = jnp.stack([shifted(mine, "tensor", 4, s) for s in range(1, 4)])
    nx = swap2(three, "xx")
    ny = swap2(three, "yy")
    nxy = swap2(nx, "yy") if x_first else swap2(ny, "xx")
    return [three, nx, ny, nxy]


def add(a, b):
    return (a.astype(f32) + b.astype(f32)).astype(bf16)


def reduce_blocks(g, rest, x_first):
    if rest > 1:
        g = [lax.psum(v, "rest") for v in g]
    first, second, near, far = ("xx", "yy", 1, 2) if x_first else ("yy", "xx", 2, 1)
    own = add(g[0], swap2(g[near], first))
    side = add(g[far], swap2(g[3], first))
    own = add(own, swap2(side, second))
    total = own[0].astype(f32)
    for s in range(1, 4):
        total = total + shifted(own[s], "tensor", 4, 4 - s).astype(f32)
    return total


def on_device(
    inputs,
    norm_in,
    w_value,
    expand,
    ema_rate,
    damping,
    project,
    ema_skip,
    w_shared,
    qk_affine,
    w_reset,
    w_update,
    w_hidden,
    u_hidden,
    norm_out,
    w_in,
    w_out,
    cotangent,
    piece_starts,
):
    c = lax.axis_index("core")
    z = lax.axis_index("tensor")
    x = lax.axis_index("xx")
    q = lax.axis_index(PLANE)
    rest = lax.axis_size("rest")
    length, width = inputs.shape
    d = width * 4
    dh = d // 2
    t = length // 2

    def half(a, dim):
        n = a.shape[dim] // 2
        return lax.dynamic_slice_in_dim(a, c * n, n, dim)

    def by_rows(a):
        return a.reshape(4, a.shape[0] // 4, a.shape[1])

    def by_cols(a):
        n = a.shape[1] // 4
        return jnp.stack([a[:, i * n : (i + 1) * n] for i in range(4)])

    starts = lax.ppermute(piece_starts, GROUP, place(0))[0]
    idx = jnp.concatenate([jnp.stack([z, q, c, x]).astype(jnp.int32), starts])

    norm_in_own = lax.dynamic_slice_in_dim(norm_in, z * width, width, 0)
    mean_in, inv_in = moments(inputs, "tensor", 4)
    unit_in = (inputs - mean_in) * inv_in
    normed = unit_in * norm_in_own
    par = jnp.concatenate([expand.T, ema_rate.T, damping.T, project.T], 0)
    skip = ema_skip[None, :]
    nb = to_chips(normed.astype(bf16))
    mixed, mixer_low, s0 = ema_fwd(normed, par, skip)
    mb = to_chips(mixer_low)

    lv = by_rows(half(w_value, 1))
    k = w_reset.shape[0]
    vq = w_reset.shape[1] // 4
    wr4 = lax.dynamic_slice_in_dim(w_reset.reshape(k, 4, vq), c * (vq // 2), vq // 2, 2)
    lp = jnp.concatenate(
        [jnp.moveaxis(wr4, 1, 0), by_cols(half(w_update, 1)), by_cols(half(w_hidden, 1))], 2
    )
    lu = by_cols(half(u_hidden, 0))
    li = by_rows(half(w_in, 1))
    lo = by_cols(half(w_out, 0))
    wv = [lv] + gather(lv, q, True)
    wsh = [w_shared] + [shifted(w_shared, "tensor", 4, s) for s in range(1, 4)]
    wp = [lp] + gather(lp, q, False)
    wu = [lu] + gather(lu, q, True)
    wi = [li] + gather(li, q, False)
    wo = [lo] + gather(lo, q, True)

    x_sp = to_chips(inputs)
    x_sp = pick(x == 0, x_sp[0], x_sp[1], 1)
    cot = to_chips(cotangent)
    cot = pick(x == 0, cot[0], cot[1], 1)
    cot_low = cot.astype(bf16)
    cot_other = swap2(cot_low, "core")

    nf, value_pre, values = call(
        value_kernel,
        [shape((t, d), bf16), shape((t, d), f32), shape((t, d), bf16)],
        idx, *nb, *[swap2(b, "core") for b in nb], *wv, name="value",
    )
    values_n = swap2(values, "xx")
    mf, reset, update, hidden, shp, qs, ks = call(
        proj_kernel,
        [
            shape((t, d), bf16), shape((t, d), f32), shape((t, dh), f32), shape((t, dh), f32),
            shape((t, 128), f32), shape((t, 128), bf16), shape((t, 128), bf16),
        ],
        idx, *mb, *[swap2(b, "core") for b in mb], *wp, *wsh, qk_affine, name="proj",
    )
    ks_n = swap2(ks, "xx")
    probs, att, gated, own, send = call(
        attend_kernel,
        [
            shape((t, 2 * t), bf16), shape((t, d), f32), shape((t, d), bf16),
            shape((t, dh), f32), shape((t, dh), bf16),
        ],
        idx, qs, ks, ks_n, values, values_n, reset, *wu, name="attend",
        scratch=[pltpu.VMEM((t, d), f32)],
    )
    gain = lax.dynamic_slice_in_dim(norm_out, c * dh, dh, 0)[None, :]
    half_f = shape((t, dh), f32)
    half_b = shape((t, dh), bf16)
    stat = shape((t, 128), f32)
    hpre, state, st = call(
        state_kernel, [half_f, half_f, stat], idx, hidden, own, swap2(send, "core"), update, x_sp, name="state"
    )
    so = swap2(st, "core")
    (low,) = call(unit_kernel, [half_b], idx, state, st, so, gain, name="unit")

    sf, gf, ffn_low, gffn, own, send = call(
        ffn_kernel,
        [shape((t, d), bf16), shape((t, d), bf16), shape((t, 2 * d), bf16), shape((t, 2 * d), bf16), half_f, half_b],
        idx, low, swap2(low, "core"), cot_low, cot_other, *wi, *wo, name="ffn",
        scratch=[pltpu.VMEM((t, d), f32)],
    )
    gunit, st2, gno = call(
        grad_unit_kernel, [half_f, stat, shape((1, dh), f32)],
        idx, own, swap2(send, "core"), state, st, so, gain, name="grad_unit",
    )
    ug, hg, gi = call(
        grad_state_kernel, [half_b, half_b, half_f],
        idx, gunit, state, st, so, st2, swap2(st2, "core"), gain, cot, hpre, update, x_sp, name="grad_state",
    )
    gi_direct = from_chips(gi)
    own, send = call(
        branch_kernel, [half_f, half_b], idx, ffn_low, *wo, name="branch", scratch=[pltpu.VMEM((t, d), f32)]
    )
    outputs = from_chips(state + own + swap2(send, "core").astype(f32))

    def blocks(r, m):
        return [shape((4, r, m), bf16)] * 4

    g_wo = call(grad_out_kernel, blocks(512, 256), idx, ffn_low, gf, name="grad_w_out")
    g_wi = call(grad_in_kernel, blocks(256, 512), idx, sf, gffn, name="grad_w_in")
    r_wo = reduce_blocks(g_wo, rest, True)
    r_wi = reduce_blocks(g_wi, rest, False)

    hf, cat, gatt, vsend = call(
        gate_kernel,
        [shape((t, d), bf16), shape((4, t, 512), bf16), shape((t, d), bf16), shape((t, d), bf16)],
        idx, hg, swap2(hg, "core"), ug, reset, att, probs, *wu, name="gate",
        scratch=[pltpu.VMEM((t, d), bf16)],
    )
    vrecv = swap2(vsend, "xx")
    qg, kown, ksend, vown = call(
        attend_back_kernel,
        [shape((t, 128), f32), shape((t, 128), f32), shape((t, 128), bf16), shape((t, d), f32)],
        idx, probs, gatt, values, values_n, ks, ks_n, qs, name="attend_back",
    )
    g_uh = call(grad_u_kernel, blocks(256, 256), idx, gated, hf, name="grad_u_hidden")
    g_pk = call(grad_pack_kernel, blocks(256, 512), idx, mf, cat, name="grad_pack")
    r_uh = reduce_blocks(g_uh, rest, True)
    r_pk = reduce_blocks(g_pk, rest, False)
    gs, ga, own, send = call(
        mixer_back_kernel,
        [shape((t, 128), bf16), shape((3, 128), f32), half_f, half_b],
        idx, cat, *wp, *wsh, qk_affine, shp, qg, kown, swap2(ksend, "xx"), name="mixer_back",
        scratch=[pltpu.VMEM((t, d), f32)],
    )
    grad_mixer = from_chips((own + swap2(send, "core").astype(f32)).astype(bf16))
    gv, own, send = call(
        value_back_kernel, [shape((t, d), bf16), half_f, half_b],
        idx, vown, vrecv, value_pre, *wv, name="value_back", scratch=[pltpu.VMEM((t, d), f32)],
    )
    normed_part = from_chips((own + swap2(send, "core").astype(f32)).astype(bf16))
    *g_wv, g_ws = call(
        grad_value_kernel, blocks(256, 256) + [shape((d, 128), f32)], idx, nf, gv, mf, gs, name="grad_w_value"
    )
    r_wv = reduce_blocks(g_wv, rest, True)

    ema_grad, g_par = ema_bwd(grad_mixer, mixed, normed, par, skip, s0)
    grad_normed = normed_part.astype(f32) + ema_grad
    g_norm_in = jnp.sum(grad_normed * unit_in, axis=0)
    gn = grad_normed * norm_in_own
    sums = sum_over(jnp.stack([jnp.sum(gn, 1), jnp.sum(gn * unit_in, 1)]), "tensor", 4) / d
    grad_inputs = gi_direct + inv_in * (gn - sums[0][:, None] - unit_in * sums[1][:, None])

    near = ("core", "xx", "yy")
    small = sum_devices(jnp.concatenate([g_par, g_norm_in[None, :]], 0), rest, near)
    wide = jnp.concatenate(
        [lax.dynamic_update_slice(jnp.zeros((d,), f32), gno[0], (c * dh,)), ga.reshape(-1)]
    )
    wide = sum_devices(wide.reshape(-1, 128), rest, near + ("tensor",)).reshape(-1)
    gno = lax.dynamic_slice_in_dim(wide, z * width, width, 0)
    gaff = wide[d:].reshape(3, -1)

    g_ws = g_ws.astype(bf16).reshape(4, width, 128)
    part = lax.dynamic_index_in_dim(g_ws, z, 0, False).astype(f32)
    for s in range(1, 4):
        part = part + shifted(
            lax.dynamic_index_in_dim(g_ws, (z + s) % 4, 0, False), "tensor", 4, s
        ).astype(f32)
    part = sum_devices(part, rest, near)
    dp = rest * 8
    me = lax.axis_index(DPS)
    o_ws = lax.dynamic_slice_in_dim(part, me * (128 // dp), 128 // dp, 1)

    r = lax.axis_index("rest")

    def swap_join(g, dim, other):
        if rest > 1:
            n = g.shape[dim] // rest
            g = lax.dynamic_slice_in_dim(g, r * n, n, dim)
        n = g.shape[dim] // 2
        keep = lax.dynamic_slice_in_dim(g, c * n, n, dim)
        send = lax.dynamic_slice_in_dim(g, (1 - c) * n, n, dim)
        return pick(c == 0, keep, swap2(send, "core"), other)

    o_wv = swap_join(r_wv, 0, 1)
    o_wi = swap_join(r_wi, 0, 1)
    o_wo = swap_join(r_wo, 1, 0)
    o_uh = swap_join(r_uh, 1, 0)
    o_wr, both = r_pk[:, 0:256], r_pk[:, 256:512]
    if rest > 1:
        n = o_wr.shape[1] // rest
        o_wr = lax.all_gather(o_wr, "core", axis=1, tiled=True)
        o_wr = lax.dynamic_slice_in_dim(o_wr, (r * 2 + c) * n, n, 1)
        pair = [lax.all_gather(v, ("core",) + PLANE, axis=1, tiled=True) for v in (both[:, 0:128], both[:, 128:256])]
        o_wu, o_wh = [lax.dynamic_slice_in_dim(v, me * (d // dp), d // dp, 1) for v in pair]
    else:
        both = lax.ppermute(both, PLANE + ("core",), [(b % 4 * 2 + b // 4, b) for b in range(8)])
        o_wu, o_wh = both[:, 0:128], both[:, 128:256]
    return (
        outputs,
        grad_inputs,
        small[72],
        o_wv,
        small[0:16].T,
        small[16:32].T,
        small[32:48].T,
        small[48:64].T,
        small[64],
        o_ws,
        gaff,
        o_wr,
        o_wu,
        o_wh,
        o_uh,
        gno,
        o_wi,
        o_wo,
    )


def solution(mesh):
    devices = np.asarray(mesh.devices)
    dp, tensor = devices.shape
    inner = Mesh(devices.reshape(2, 2, dp // 8, 2, tensor), ALL)
    t = "tensor"
    placed = (
        P(DPS, t),
        P(),
        P(None, t),
        P(t, None),
        P(t, None),
        P(t, None),
        P(t, None),
        P(t),
        P(t, None),
        P(),
        P(t, None),
        P(t, None),
        P(t, None),
        P(t, None),
        P(),
        P(None, t),
        P(t, None),
        P(DPS, t),
        P(DPS, None),
    )
    return jax.shard_map(
        on_device,
        mesh=inner,
        in_specs=placed,
        out_specs=(
            P(DPS, t),
            P(DPS, t),
            P(t),
            P(DPS, t),
            P(t, None),
            P(t, None),
            P(t, None),
            P(t, None),
            P(t),
            P(t, DPS),
            P(),
            P(t, DPS),
            P(t, DPS),
            P(t, DPS),
            P(t, DPS),
            P(t),
            P(DPS, t),
            P(t, DPS),
        ),
        check_vma=False,
    )
```

```python
import jax
import jax.numpy as jnp
import numpy as np
from jax import lax
from jax.experimental import pallas as pl
from jax.experimental.pallas import tpu as pltpu
from jax.sharding import Mesh, PartitionSpec as P

f32 = jnp.float32
bf16 = jnp.bfloat16
PIECE = 256
EPS = 1e-5
HD = 16
CH = 8
LT = 128

GROUP = ("xx", "core", "tensor")
PLANE = ("yy", "xx")
DPS = ("yy", "xx", "rest", "core")
ALL = DPS + ("tensor",)

VM = pl.BlockSpec(memory_space=pltpu.VMEM)
SM = pl.BlockSpec(memory_space=pltpu.SMEM)


def shape(dims, dtype):
    return jax.ShapeDtypeStruct(tuple(dims), dtype)


def call(body, outs, idx, *args, name, scratch=(), flops=0, limit=48):
    return pl.pallas_call(
        body,
        out_shape=tuple(outs),
        in_specs=[SM] + [VM] * len(args),
        out_specs=(VM,) * len(outs),
        scratch_shapes=list(scratch),
        name=name,
        compiler_params=pltpu.CompilerParams(vmem_limit_bytes=limit << 20),
    )(idx, *args)


def dot(a, b):
    return jnp.dot(a, b, preferred_element_type=f32)


def dot_t(a, b):
    return lax.dot_general(a, b, (((1,), (1,)), ((), ())), preferred_element_type=f32)


def t_dot(a, b):
    return lax.dot_general(a, b, (((0,), (0,)), ((), ())), preferred_element_type=f32)


def sig(v):
    return 1.0 / (1.0 + jnp.exp(-v))


def silu(v):
    return v * sig(v)


def silu_grad(v):
    s = sig(v)
    return s * (1.0 + v * (1.0 - s))


def at(i, n):
    return pl.ds(pl.multiple_of(i * n, n), n)


def _params(par_ref, lanes):
    expand = par_ref[0:16, lanes]; rate = par_ref[16:32, lanes]
    damp = par_ref[32:48, lanes]; proj = par_ref[48:64, lanes]
    dec = 1.0 - rate*damp
    coef = proj*rate*expand
    return expand, rate, damp, proj, dec, coef

def _rows(a):
    return [jnp.broadcast_to(a[h:h+1], (CH, LT)) for h in range(HD)]

def _pow(a, n):
    out=None; base=a
    while n:
        if n&1: out = base if out is None else out*base
        n >>= 1
        if n: base = base*base
    return out

def _carry_down(s, decl):
    row = lax.broadcasted_iota(jnp.int32, (CH, LT), 0)
    out=[]
    for h in range(HD):
        v = s[h]; p = decl[h]
        for d in (1,2,4):
            v = v + p*jnp.where(row >= d, pltpu.roll(v, d, 0), 0.0)
            p = p*p
        out.append(jnp.where(row >= 1, pltpu.roll(v, 1, 0), 0.0))
    return out

def _carry_up(s, decl):
    row = lax.broadcasted_iota(jnp.int32, (CH, LT), 0)
    out=[]
    for h in range(HD):
        v = s[h]; p = decl[h]
        for d in (1,2,4):
            v = v + p*jnp.where(row < CH-d, pltpu.roll(v, CH-d, 0), 0.0)
            p = p*p
        out.append(jnp.where(row < CH-1, pltpu.roll(v, CH-1, 0), 0.0))
    return out

def fwd_kernel(x_ref, par_ref, skip_ref, m_ref, low_ref, s0_ref, xs, ms):
    T, W = x_ref.shape
    L = T//CH
    for lt in range(W//LT):
        lanes = slice(lt*LT, (lt+1)*LT)
        *_, dec, coef = _params(par_ref, lanes)
        dec = _rows(dec); coef=_rows(coef)
        skip = jnp.broadcast_to(skip_ref[0:1, lanes], (CH, LT))
        z = jnp.zeros((CH,LT), f32)
        xs[...] = x_ref[:, lanes]
        def one(i, s):
            xi = xs[pl.ds(i, CH, stride=L), :]
            return tuple(dec[h]*s[h]+xi for h in range(HD))
        s = lax.fori_loop(0, L, one, (z,)*HD, unroll=8)
        s0 = _carry_down(s, [_pow(dec[h], L) for h in range(HD)])
        for h in range(HD):
            s0_ref[h, :, lanes] = s0[h]
        def two(i, s):
            xi = xs[pl.ds(i, CH, stride=L), :]
            s = tuple(dec[h]*s[h]+xi for h in range(HD))
            y = skip*xi
            terms=[coef[h]*s[h] for h in range(HD)]
            while len(terms)>1:
                terms=[terms[k]+terms[k+1] for k in range(0,len(terms),2)]
            ms[pl.ds(i, CH, stride=L), :] = y+terms[0]
            return s
        lax.fori_loop(0, L, two, tuple(s0), unroll=4)
        m_ref[:, lanes] = ms[...]
        low_ref[:, lanes] = xs[...].astype(bf16)
        low_ref[:, W + lt*LT : W + (lt+1)*LT] = silu(ms[...]).astype(bf16)

def bwd_kernel(g_ref, m_ref, x_ref, par_ref, skip_ref, s0_ref, eg_ref, gp_ref, gm_ref, st_ref, xs, gs_ref, es):
    T, W = x_ref.shape
    L = T//CH
    for lt in range(W//LT):
        lanes = slice(lt*LT, (lt+1)*LT)
        expand, rate, damp, proj, dec2, coef2 = _params(par_ref, lanes)
        dec=_rows(dec2); coef=_rows(coef2)
        skip = jnp.broadcast_to(skip_ref[0:1, lanes], (CH, LT))
        z = jnp.zeros((CH,LT), f32)
        xs[...] = x_ref[:, lanes]
        m = m_ref[:, lanes]
        sg = 1.0/(1.0+jnp.exp(-m))
        gs_ref[...] = g_ref[:, lanes].astype(f32)*(sg*(1.0+m*(1.0-sg)))
        def one(k, c):
            b, gs = c
            i = L-1-k
            gm = gs_ref[pl.ds(i, CH, stride=L), :]
            gm_ref[i] = gm
            xi = xs[pl.ds(i, CH, stride=L), :]
            gs = gs + gm*xi
            return (tuple(dec[h]*b[h]+gm for h in range(HD)), gs)
        b, gs = lax.fori_loop(0, L, one, ((z,)*HD, z), unroll=4)
        e = _carry_up(b, [_pow(dec[h], L) for h in range(HD)])
        s0 = [s0_ref[h, :, lanes] for h in range(HD)]
        for h in range(HD): st_ref[0, h] = s0[h]
        def rec(i, s):
            xi = xs[pl.ds(i, CH, stride=L), :]
            s = tuple(dec[h]*s[h]+xi for h in range(HD))
            for h in range(HD): st_ref[i+1, h] = s[h]
            return s
        lax.fori_loop(0, L, rec, tuple(s0), unroll=4)
        gcoef=[]; gdec=[]
        G=8
        for g0 in range(0, HD, G):
            hs = range(g0, g0+G)
            def two(k, c):
                b, gc, gd = c
                i = L-1-k
                gm = gm_ref[i]
                b = tuple(dec[h]*b[j]+gm for j,h in enumerate(hs))
                gc = tuple(gc[j]+gm*st_ref[i+1,h] for j,h in enumerate(hs))
                gd = tuple(gd[j]+b[j]*st_ref[i,h] for j,h in enumerate(hs))
                terms=[coef[h]*b[j] for j,h in enumerate(hs)]
                while len(terms)>1:
                    terms=[terms[q]+terms[q+1] for q in range(0,len(terms),2)]
                if g0==0: base = skip*gm
                else: base = es[pl.ds(i, CH, stride=L), :]
                es[pl.ds(i, CH, stride=L), :] = base+terms[0]
                return (b, gc, gd)
            zz=(z,)*G
            _, gc, gd = lax.fori_loop(0, L, two, (tuple(e[h] for h in hs), zz, zz), unroll=2)
            gcoef += list(gc); gdec += list(gd)
        eg_ref[:, lanes] = es[...]
        gcoef = jnp.concatenate([jnp.sum(v,0,keepdims=True) for v in gcoef],0)
        gdec = jnp.concatenate([jnp.sum(v,0,keepdims=True) for v in gdec],0)*coef2
        gp_ref[0:16, lanes] = gcoef*proj*rate
        gp_ref[16:32, lanes] = gcoef*proj*expand - gdec*damp
        gp_ref[32:48, lanes] = -gdec*rate
        gp_ref[48:64, lanes] = gcoef*rate*expand
        gp_ref[64:72, lanes] = jnp.broadcast_to(jnp.sum(gs,0,keepdims=True),(8,LT))

def ema_fwd(x, par, skip):
    T,W = x.shape
    return pl.pallas_call(fwd_kernel, out_shape=(jax.ShapeDtypeStruct((T,W),f32), jax.ShapeDtypeStruct((T,2*W),bf16), jax.ShapeDtypeStruct((HD,CH,W),f32)),
        in_specs=[VM]*3, out_specs=(VM,VM,VM), name="ema_fwd", scratch_shapes=[pltpu.VMEM((T,LT),f32)]*2,
        compiler_params=pltpu.CompilerParams(vmem_limit_bytes=48<<20))(x,par,skip)
def ema_bwd(g,m,x,par,skip,s0):
    T,W = x.shape
    return pl.pallas_call(bwd_kernel, out_shape=(jax.ShapeDtypeStruct((T,W),f32), jax.ShapeDtypeStruct((72,W),f32)),
        in_specs=[VM]*6, out_specs=(VM,VM), name="ema_bwd",
        scratch_shapes=[pltpu.VMEM((T//CH,CH,LT),f32), pltpu.VMEM((T//CH+1,HD,CH,LT),f32)]+[pltpu.VMEM((T,LT),f32)]*3,
        compiler_params=pltpu.CompilerParams(vmem_limit_bytes=48<<20))(g,m,x,par,skip,s0)


def tile(loc, rem, q, rel, s, pick=None):
    if s == 0:
        return loc[q ^ rel]
    return rem[rel][s - 1] if pick is None else rem[rel][s - 1, pick]


def value_kernel(idx, n0, n1, o0, o1, gain, st, loc, r0, r1, r2, r3, full, pre, val, xs):
    z, q, c, x = idx[0], idx[1], idx[2], idx[3]
    rem = (r0, r1, r2, r3)
    full[:, at(2 * c + x, 256)] = n0[:, 0:256]
    full[:, at(2 * c + 1 - x, 256)] = n1[:, 0:256]
    full[:, at(2 - 2 * c + x, 256)] = o0[:, 0:256]
    full[:, at(3 - 2 * c - x, 256)] = o1[:, 0:256]
    for j, v in enumerate((n0, n1)):
        b = x if j == 0 else 1 - x
        xs[:, at(b, 256)] = v[:, 0:256].astype(f32) / gain[:, at(2 * c + b, 256)] * st[:, 1:2] + st[:, 0:1]
    for s in range(4):
        acc = None
        for rel in range(4):
            t = dot(full[:, at(q ^ rel, 256)], tile(loc, rem, q, rel, s, 0))
            acc = t if acc is None else acc + t
        v = at(lax.rem(z + 4 - s, 4), 256)
        pre[:, v] = acc
        val[:, v] = silu(acc).astype(bf16)


def proj_kernel(
    idx, n0, n1, o0, o1, loc, r0, r1, r2, r3, ws, aff,
    full, reset, update, hidden, shp, qs, ks,
):
    z, q, c, x = idx[0], idx[1], idx[2], idx[3]
    rem = (r0, r1, r2, r3)
    full[:, at(2 * c + x, 256)] = n0[:, 256:512]
    full[:, at(2 * c + 1 - x, 256)] = n1[:, 256:512]
    full[:, at(2 - 2 * c + x, 256)] = o0[:, 256:512]
    full[:, at(3 - 2 * c - x, 256)] = o1[:, 256:512]
    rows = [full[:, at(lax.rem(z + 4 - s, 4), 256)] for s in range(4)]
    acc = None
    for s in range(4):
        t = dot(rows[s], ws[lax.rem(z + 4 - s, 4)])
        acc = t if acc is None else acc + t
    shp[...] = acc
    sh = silu(acc)
    qs[...] = (sh * aff[0:1, :] + aff[1:2, :]).astype(bf16)
    ks[...] = (sh * aff[2:3, :]).astype(bf16)
    for rel in range(4):
        acc = None
        for s in range(4):
            t = dot(rows[s], tile(loc, rem, q, rel, s))
            acc = t if acc is None else acc + t
        b = q ^ rel
        reset[:, at(b, 256)] = acc[:, 0:256]
        update[:, at(b, 128)] = acc[:, 256:384]
        hidden[:, at(b, 128)] = acc[:, 384:512]


def attend_kernel(
    idx, qs, ko, kn, vo, vn, reset, loc, r0, r1, r2, r3, probs, att, gated, own, send, part,
):
    z, q, c, x = idx[0], idx[1], idx[2], idx[3]
    rem = (r0, r1, r2, r3)
    t = qs.shape[0]
    scale = qs.shape[1] ** (-0.5)
    tm = 256
    for i in range(t // tm):
        r = slice(i * tm, (i + 1) * tm)
        row = x * t + i * tm + lax.broadcasted_iota(jnp.int32, (tm, t), 0)
        parts = []
        for k, half in ((ko, x), (kn, 1 - x)):
            col = half * t + lax.broadcasted_iota(jnp.int32, (tm, t), 1)
            seen = col <= row
            for n in range(2):
                first = idx[4 + n]
                lo = jnp.minimum(row, col) >= first
                hi = jnp.maximum(row, col) < first + PIECE
                seen = seen | (lo & hi)
            parts.append(jnp.where(seen, dot_t(qs[r, :], k[...]) * scale, -1e30))
        top = jnp.maximum(
            jnp.max(parts[0], axis=1, keepdims=True), jnp.max(parts[1], axis=1, keepdims=True)
        )
        e = [jnp.exp(p - top) for p in parts]
        total = jnp.sum(e[0], axis=1, keepdims=True) + jnp.sum(e[1], axis=1, keepdims=True)
        inv = 1.0 / total
        p = [(v * inv).astype(bf16) for v in e]
        probs[r, 0:t] = p[0]
        probs[r, t : 2 * t] = p[1]
        a = dot(p[0], vo[...]) + dot(p[1], vn[...])
        att[r, :] = a
        gated[r, :] = (silu(reset[r, :]) * a).astype(bf16)
    for rel in range(4):
        acc = None
        for s in range(4):
            v = dot(gated[:, at(lax.rem(z + 4 - s, 4), 256)], tile(loc, rem, q, rel, s, 1))
            acc = v if acc is None else acc + v
        part[:, at(q ^ rel, 256)] = acc
    own[...] = part[:, at(c, 512)]
    send[...] = part[:, at(1 - c, 512)].astype(bf16)


def state_kernel(idx, hidden, own, recv, upd, xs, hpre, state, st):
    h = hidden[...] + own[...] + recv[...].astype(f32)
    hpre[...] = h
    u = sig(upd[...])
    v = u * silu(h) + (1.0 - u) * xs[...]
    state[...] = v
    mean = jnp.mean(v, axis=1, keepdims=True)
    second = jnp.sum(jnp.square(v - mean), axis=1, keepdims=True)
    lane = lax.broadcasted_iota(jnp.int32, st.shape, 1)
    st[...] = jnp.where(lane < 64, mean, second)


def unit_of(state, st, so):
    w = state.shape[1]
    m0, m1 = st[:, 0:1], so[:, 0:1]
    mean = 0.5 * (m0 + m1)
    total = st[:, 64:65] + so[:, 64:65] + w * (jnp.square(m0 - mean) + jnp.square(m1 - mean))
    inv = lax.rsqrt(total / (2 * w) + EPS)
    return (state[...] - mean) * inv, inv


def unit_kernel(idx, state, st, so, gain, low):
    unit, _ = unit_of(state, st, so)
    low[...] = (unit * gain[...]).astype(bf16)


def join(full, a, b, c):
    w = a.shape[1]
    full[:, at(c, w)] = a[...]
    full[:, at(1 - c, w)] = b[...]


def quad(loc, rem, y, rel, s):
    return loc[y ^ rel] if s == 0 else rem[rel][s - 1]


def ffn_kernel(
    idx, s0, s1, s2, s3, g0, g1, g2, g3, il, i0, i1, ol, o0, o1, sf, gf, low, gffn, top, bot, send, part,
):
    y, c = idx[1] >> 1, idx[2]
    t = s0.shape[0]
    for full, blocks in ((sf, (s0, s1, s2, s3)), (gf, (g0, g1, g2, g3))):
        for n, v in enumerate(blocks):
            full[n // 2 * t : (n // 2 + 1) * t, at(1 - c if n % 2 else c, 512)] = v[...]
    for s in range(4):
        f = slice(s * 256, (s + 1) * 256)
        pre = dot(sf[:, at(y, 512)], quad(il, (i0, i1), y, 0, s))
        pre = pre + dot(sf[:, at(1 - y, 512)], quad(il, (i0, i1), y, 1, s))
        low[:, f] = silu(pre).astype(bf16)
        g = dot_t(gf[:, at(y, 512)], quad(ol, (o0, o1), y, 0, s))
        g = g + dot_t(gf[:, at(1 - y, 512)], quad(ol, (o0, o1), y, 1, s))
        gffn[:, f] = (g * silu_grad(pre)).astype(bf16)
    for rel in range(2):
        acc = None
        for s in range(4):
            v = dot_t(gffn[:, s * 256 : (s + 1) * 256], quad(il, (i0, i1), y, rel, s))
            acc = v if acc is None else acc + v
        part[y ^ rel] = acc
    top[...] = part[c, 0:t]
    bot[...] = part[c, t : 2 * t]
    send[...] = part[1 - c].astype(bf16)


def branch_kernel(idx, low, ol, o0, o1, top, bot, send, part):
    y, c = idx[1] >> 1, idx[2]
    t = top.shape[0]
    for rel in range(2):
        acc = None
        for s in range(4):
            v = dot(low[:, s * 256 : (s + 1) * 256], quad(ol, (o0, o1), y, rel, s))
            acc = v if acc is None else acc + v
        part[y ^ rel] = acc
    top[...] = part[c, 0:t]
    bot[...] = part[c, t : 2 * t]
    send[...] = part[1 - c].astype(bf16)


def grad_ffn_kernel(idx, low, gf, sf, gffn, keep, send):
    z, y = idx[0], idx[1] >> 1
    for n, (a, b) in enumerate(((low, gf), (gffn, sf))):
        for s in range(4):
            v = a[:, s * 256 : (s + 1) * 256]
            p = lax.rem(z + 4 - s, 4)
            keep[p, n] = t_dot(v, b[:, at(y, 512)]).astype(bf16)
            send[p, n] = t_dot(v, b[:, at(1 - y, 512)]).astype(bf16)


def grad_unit_kernel(idx, own, recv, xrecv, state, st, so, gain, gu, st2, gno):
    unit, _ = unit_of(state, st, so)
    g = own[...] + recv[0 : own.shape[0], :].astype(f32) + xrecv[...].astype(f32)
    gu[...] = g
    gno[...] = jnp.sum(g * unit, axis=0, keepdims=True)
    gn = g * gain[...]
    lane = lax.broadcasted_iota(jnp.int32, st2.shape, 1)
    st2[...] = jnp.where(
        lane < 64, jnp.sum(gn, axis=1, keepdims=True), jnp.sum(gn * unit, axis=1, keepdims=True)
    )


def grad_state_kernel(idx, gu, state, st, so, t0, t1, gain, cot, hpre, upd, xs, ug, hg, gi):
    unit, inv = unit_of(state, st, so)
    d = 2 * state.shape[1]
    m1 = (t0[:, 0:1] + t1[:, 0:1]) / d
    m2 = (t0[:, 64:65] + t1[:, 64:65]) / d
    gs = cot[...] + inv * (gu[...] * gain[...] - m1 - unit * m2)
    u = sig(upd[...])
    h = hpre[...]
    s = sig(h)
    ug[...] = (gs * (h * s - xs[...]) * u * (1.0 - u)).astype(bf16)
    hg[...] = (gs * u * (s * (1.0 + h * (1.0 - s)))).astype(bf16)
    gi[...] = (gs * (1.0 - u)).astype(bf16)


def gate_kernel(
    idx, h0, h1, ug, reset, att, probs, loc, r0, r1, r2, r3, hf, cat, gatt, vsend, gr,
):
    z, q, c = idx[0], idx[1], idx[2]
    rem = (r0, r1, r2, r3)
    t = h0.shape[0]
    join(hf, h0, h1, c)
    for s in range(4):
        v = at(lax.rem(z + 4 - s, 4), 256)
        g = None
        for rel in range(4):
            w = dot_t(hf[:, at(q ^ rel, 256)], tile(loc, rem, q, rel, s, 1))
            g = w if g is None else g + w
        r = reset[:, v]
        sg = sig(r)
        gatt[:, v] = (g * (r * sg)).astype(bf16)
        gr[:, v] = (g * att[:, v] * (sg * (1.0 + r * (1.0 - sg)))).astype(bf16)
    for rel in range(4):
        b = q ^ rel
        cat[rel, :, 0:256] = gr[:, at(b, 256)]
        cat[rel, :, 256:384] = ug[:, at(b, 128)]
        cat[rel, :, 384:512] = h0[:, at(b, 128)]
    vsend[...] = t_dot(probs[:, t : 2 * t], gatt[...]).astype(bf16)


def attend_back_kernel(idx, probs, gatt, vo, vn, ko, kn, qs, qg, kown, ksend, vown):
    t = qs.shape[0]
    scale = qs.shape[1] ** (-0.5)
    p = [probs[:, 0:t].astype(f32), probs[:, t : 2 * t].astype(f32)]
    g = [dot_t(gatt[...], vo[...]), dot_t(gatt[...], vn[...])]
    center = jnp.sum(p[0] * g[0], axis=1, keepdims=True) + jnp.sum(p[1] * g[1], axis=1, keepdims=True)
    gs = [(a * (b - center) * scale).astype(bf16) for a, b in zip(p, g)]
    ksend[...] = t_dot(gs[1], qs[...]).astype(bf16)
    qg[...] = dot(gs[0], ko[...]) + dot(gs[1], kn[...])
    kown[...] = t_dot(gs[0], qs[...])
    vown[...] = t_dot(probs[:, 0:t], gatt[...])


def mixer_back_kernel(
    idx, vown, recv, pre, vloc, v0, v1, v2, v3, cat, loc, r0, r1, r2, r3, ws, aff, shp, qg, kown,
    gv, gs, ga, own, send, part,
):
    z, q, c = idx[0], idx[1], idx[2]
    rem = (r0, r1, r2, r3)
    d = vown.shape[1]
    gv[...] = ((vown[...] + recv[:, 0:d].astype(f32)) * silu_grad(pre[...])).astype(bf16)
    for rel in range(4):
        acc = None
        for s in range(4):
            w = dot_t(gv[:, at(lax.rem(z + 4 - s, 4), 256)], tile(vloc, (v0, v1, v2, v3), q, rel, s, 0))
            acc = w if acc is None else acc + w
        part[:, at(q ^ rel, 256)] = acc
    own[1] = part[:, at(c, 512)]
    send[1] = part[:, at(1 - c, 512)].astype(bf16)
    kg = kown[...] + recv[:, d:].astype(f32)
    s_pre = shp[...]
    sh = silu(s_pre)
    g = qg[...]
    gs[...] = ((g * aff[0:1, :] + kg * aff[2:3, :]) * silu_grad(s_pre)).astype(bf16)
    rows = [jnp.sum(v, axis=0, keepdims=True) for v in (g * sh, g, kg * sh)]
    ga[...] = jnp.concatenate(rows + [jnp.zeros((5, g.shape[1]), f32)], 0)
    for s in range(4):
        acc = dot_t(gs[...], ws[lax.rem(z + 4 - s, 4)])
        for rel in range(4):
            acc = acc + dot_t(cat[rel], tile(loc, rem, q, rel, s))
        part[:, at(lax.rem(z + 4 - s, 4), 256)] = acc
    own[0] = part[:, at(c, 512)]
    send[0] = part[:, at(1 - c, 512)].astype(bf16)


def grad_pack_kernel(idx, mf, cat, keep, send):
    z = idx[0]
    for s in range(4):
        a = mf[:, at(lax.rem(z + 4 - s, 4), 256)]
        for rel in range(4):
            out = send if rel & 2 else keep
            out[rel & 1, lax.rem(z + 4 - s, 4)] = t_dot(a, cat[rel]).astype(bf16)


def grad_u_kernel(idx, gated, hf, keep, send):
    z, q = idx[0], idx[1]
    for s in range(4):
        a = gated[:, at(lax.rem(z + 4 - s, 4), 256)]
        for rel in range(4):
            out = send if rel & 1 else keep
            out[rel >> 1, lax.rem(z + 4 - s, 4)] = t_dot(a, hf[:, at(q ^ rel, 256)]).astype(bf16)


def grad_value_kernel(idx, nf, gv, mf, gs, keep, send, gws):
    z, q = idx[0], idx[1]
    for rel in range(4):
        a = nf[:, at(q ^ rel, 256)]
        for s in range(4):
            out = send if rel & 1 else keep
            out[rel >> 1, lax.rem(z + 4 - s, 4)] = t_dot(a, gv[:, at(lax.rem(z + 4 - s, 4), 256)]).astype(bf16)
    gws[...] = t_dot(mf[...], gs[...])


def place(k):
    return [
        ((x * 2 + c) * 4 + z, (((z + k) % 2) * 2 + z // 2) * 4 + 2 * x + c)
        for x in range(2)
        for c in range(2)
        for z in range(4)
    ]


def pick(pred, a, b, axis):
    return jnp.where(pred, jnp.concatenate([a, b], axis), jnp.concatenate([b, a], axis))


def to_chips(a):
    z = lax.axis_index("tensor")
    halves = a.reshape(2, a.shape[0] // 2, a.shape[1])
    return [
        lax.ppermute(lax.dynamic_index_in_dim(halves, (z + k) % 2, 0, False), GROUP, place(k))
        for k in range(2)
    ]


def from_chips(a):
    z = lax.axis_index("tensor")
    x = lax.axis_index("xx")
    w = a.shape[1] // 2
    r = [
        lax.ppermute(
            lax.dynamic_slice_in_dim(a, ((x + k) % 2) * w, w, 1),
            GROUP,
            [(t, s) for s, t in place(k)],
        )
        for k in range(2)
    ]
    return pick(z % 2 == 0, r[0], r[1], 0)


def after(v, *deps):
    return lax.optimization_barrier((v,) + deps)[0]


def swap2(a, axis):
    return lax.ppermute(a, axis, [(0, 1), (1, 0)])


def shifted(a, axis, count, s):
    return lax.ppermute(a, axis, [(i, (i + s) % count) for i in range(count)])


def moments(rows, axis, count):
    width = rows.shape[1]
    mean = jnp.mean(rows, axis=1)
    second = jnp.sum(jnp.square(rows - mean[:, None]), axis=1)
    both = jnp.stack([mean, second])
    parts = [both] + [shifted(both, axis, count, s) for s in range(1, count)]
    total_mean = sum(p[0] for p in parts) / count
    total = sum(p[1] + width * jnp.square(p[0] - total_mean) for p in parts)
    return total_mean[:, None], lax.rsqrt(total / (width * count) + EPS)[:, None]


def sum_over(v, axis, count):
    return v + sum(shifted(v, axis, count, s) for s in range(1, count))


def sum_devices(v, rest, axes):
    for a in axes:
        v = v + (swap2(v, a) if a != "tensor" else sum(shifted(v, a, 4, s) for s in range(1, 4)))
    return lax.psum(v, "rest") if rest > 1 else v


def others(every, z):
    return jnp.concatenate(
        [lax.dynamic_slice_in_dim(every, (z + 4 - s) % 4, 1, 0) for s in range(1, 4)]
    )


def spread_plane(three, *deps):
    nx = swap2(three, "xx")
    ny = swap2(three, "yy")
    nxy = swap2(after(nx, *deps), "yy")
    return [three, nx, ny, nxy]


def add(a, b):
    return (a.astype(f32) + b.astype(f32)).astype(bf16)


def reduce_plane(keep, send, first, second, dep):
    pair = add(keep, after(swap2(send, first), dep))
    return add(pair[0], swap2(pair[1], second))


def reduce_tensor(own, rest):
    if rest > 1:
        own = lax.psum(own, "rest")
    return lax.psum_scatter(own, "tensor", scatter_dimension=0)


def reduce_tensor_direct(own, rest, z):
    if rest > 1:
        own = lax.psum(own, "rest")
    total = lax.dynamic_index_in_dim(own, z, 0, False).astype(f32)
    for s in range(1, 4):
        v = lax.dynamic_index_in_dim(own, (z + s) % 4, 0, False)
        total = total + shifted(v, "tensor", 4, s).astype(f32)
    return total


def on_device(
    inputs,
    norm_in,
    w_value,
    expand,
    ema_rate,
    damping,
    project,
    ema_skip,
    w_shared,
    qk_affine,
    w_reset,
    w_update,
    w_hidden,
    u_hidden,
    norm_out,
    w_in,
    w_out,
    cotangent,
    piece_starts,
):
    c = lax.axis_index("core")
    z = lax.axis_index("tensor")
    x = lax.axis_index("xx")
    q = lax.axis_index(PLANE)
    rest = lax.axis_size("rest")
    length, width = inputs.shape
    d = width * 4
    dh = d // 2
    t = length // 2

    def half(a, dim):
        n = a.shape[dim] // 2
        return lax.dynamic_slice_in_dim(a, c * n, n, dim)

    def by_rows(a):
        return a.reshape(4, a.shape[0] // 4, a.shape[1])

    def by_cols(a):
        n = a.shape[1] // 4
        return jnp.stack([a[:, i * n : (i + 1) * n] for i in range(4)])

    y = q // 2
    lv = by_rows(half(w_value, 1))
    k = w_reset.shape[0]
    vq = w_reset.shape[1] // 4
    wr4 = lax.dynamic_slice_in_dim(w_reset.reshape(k, 4, vq), c * (vq // 2), vq // 2, 2)
    lp = jnp.concatenate(
        [jnp.moveaxis(wr4, 1, 0), by_cols(half(w_update, 1)), by_cols(half(w_hidden, 1))], 2
    )
    lu = by_cols(half(u_hidden, 0))
    fq = w_in.shape[1] // 4
    li = lax.dynamic_slice_in_dim(w_in, (c * 2 + x) * fq, fq, 1).reshape(2, d // 2, fq)
    lo = lax.dynamic_slice_in_dim(w_out, (c * 2 + x) * fq, fq, 0)
    lo = jnp.stack([lo[:, : d // 2], lo[:, d // 2 :]])

    def part(a, i):
        return lax.dynamic_index_in_dim(a, i, 0, False)

    def planes(a):
        return lax.all_gather(a, "tensor", axis=0)

    nq, nc = d // 4, w_value.shape[1] // 2
    first = jnp.stack(
        [
            lax.dynamic_slice(w_value, (q * nq, c * nc), (nq, nc)),
            lax.dynamic_slice(u_hidden, (c * nc, q * nq), (nc, nq)),
        ]
    )
    norm_in_own = lax.dynamic_slice_in_dim(norm_in, z * width, width, 0)
    mean_in, inv_in = moments(after(inputs, first), "tensor", 4)
    starts = piece_starts[0].astype(f32)
    about = jnp.stack([mean_in[:, 0], 1.0 / inv_in[:, 0]])
    about = lax.dynamic_slice_in_dim(about, (z % 2) * t, t, 1)
    about = jnp.concatenate([about, jnp.pad(starts, (0, t - 2))[None]])
    unit_in = (inputs - mean_in) * inv_in
    normed = unit_in * norm_in_own
    par = jnp.concatenate([expand.T, ema_rate.T, damping.T, project.T], 0)
    skip = ema_skip[None, :]
    mixed, both_low, s0 = ema_fwd(normed, par, skip)
    nm = to_chips(both_low)
    about = lax.ppermute(about, GROUP, place(0))
    starts = about[2, 0:2].astype(jnp.int32)
    idx = jnp.concatenate([jnp.stack([z, q, c, x]).astype(jnp.int32), starts])
    about = about[0:2].T

    ac = others(planes(first), z)
    ac = spread_plane(after(ac, both_low), *nm)
    nm = nm + [swap2(after(b, ac[1], ac[2]), "core") for b in nm]
    pk = planes(after(jnp.concatenate([part(lp, q), w_shared], 1), *nm[:2]))
    wv, wu = [lv] + ac, [lu] + ac

    nf, value_pre, values, x_sp = call(
        value_kernel,
        [shape((t, d), bf16), shape((t, d), f32), shape((t, d), bf16), shape((t, dh), f32)],
        idx, *nm, norm_in[None, :], about, *wv, name="value",
    )
    values_n = swap2(values, "xx")
    ws = after(pk, values)[:, :, lp.shape[2] :]
    wp = [lp] + spread_plane(others(after(pk[:, :, : lp.shape[2]], values), z))
    cot = to_chips(after(cotangent.astype(bf16), *nm[:2]))
    cot_low = pick(x == 0, cot[0], cot[1], 1)
    cot_core = swap2(cot_low, "core")
    cot_x = swap2(after(cot_low, wp[3]), "xx")
    cots = [cot_low, cot_core, cot_x, swap2(cot_x, "core")]
    mf, reset, update, hidden, shp, qs, ks = call(
        proj_kernel,
        [
            shape((t, d), bf16), shape((t, d), f32), shape((t, dh), f32), shape((t, dh), f32),
            shape((t, 128), f32), shape((t, 128), bf16), shape((t, 128), bf16),
        ],
        idx, *nm, *wp, ws, after(qk_affine, cot_low), name="proj",
    )
    ks_n = swap2(ks, "xx")
    wi = others(after(planes(part(li, y)), qs), z)
    wi = [li, wi, swap2(wi, "yy")]
    probs, att, gated, own, send = call(
        attend_kernel,
        [
            shape((t, 2 * t), bf16), shape((t, d), f32), shape((t, d), bf16),
            shape((t, dh), f32), shape((t, dh), bf16),
        ],
        idx, qs, ks, ks_n, values, values_n, after(reset, *cots), *wu, name="attend",
        scratch=[pltpu.VMEM((t, d), f32)],
    )
    wo = others(after(planes(part(lo, y)), gated), z)
    wo = [lo, wo, swap2(wo, "yy")]
    gain = lax.dynamic_slice_in_dim(norm_out, c * dh, dh, 0)[None, :]
    half_f = shape((t, dh), f32)
    half_b = shape((t, dh), bf16)
    stat = shape((t, 128), f32)
    hpre, state, st = call(
        state_kernel, [half_f, half_f, stat], idx, hidden, own, swap2(send, "core"), update, x_sp, name="state"
    )
    so = swap2(st, "core")
    (low,) = call(unit_kernel, [half_b], idx, state, st, so, gain, name="unit")

    def blocks(r, m):
        return [shape((4, r, m), bf16)] * 4

    low_x = swap2(low, "xx")
    f_out = [half_f, half_f, shape((2 * t, dh), bf16)]
    sf, gf, ffn_low, gffn, top, bot, send = call(
        ffn_kernel,
        [shape((2 * t, d), bf16)] * 4 + f_out,
        idx, low, swap2(low, "core"), low_x, swap2(low_x, "core"), *cots, *wi, *wo, name="ffn",
        scratch=[pltpu.VMEM((2, 2 * t, dh), f32)],
    )

    def over_x(bot, recv):
        return (bot + recv[t:].astype(f32)).astype(bf16)

    recv = swap2(send, "core")
    x_send = over_x(bot, recv)
    b_top, b_bot, b_send = call(
        branch_kernel, f_out, idx, after(ffn_low, x_send), *wo, name="branch", scratch=[pltpu.VMEM((2, 2 * t, dh), f32)]
    )
    f_keep, f_send = call(
        grad_ffn_kernel, [shape((4, 2, 256, 512), bf16)] * 2, idx, ffn_low, gf, sf, after(gffn, x_send), name="grad_ffn"
    )
    f_recv = swap2(f_send, "yy")
    gunit, st2, gno = call(
        grad_unit_kernel, [half_f, stat, shape((1, dh), f32)],
        idx, after(top, b_top, f_keep), recv, swap2(x_send, "xx"), state, st, so, gain, name="grad_unit",
    )
    cot = cot_low
    ug, hg, gi = call(
        grad_state_kernel, [half_b, half_b, half_b],
        idx, gunit, state, st, so, st2, swap2(st2, "core"), gain, cot, hpre, update, x_sp, name="grad_state",
    )

    b_recv = swap2(b_send, "core")
    b_x = over_x(b_bot, b_recv)
    hf, cat, gatt, vsend = call(
        gate_kernel,
        [shape((t, d), bf16), shape((4, t, 512), bf16), shape((t, d), bf16), shape((t, d), bf16)],
        idx, hg, swap2(hg, "core"), after(ug, b_x), reset, att, probs, *wu, name="gate",
        scratch=[pltpu.VMEM((t, d), bf16)],
    )
    qg, kown, ksend, vown = call(
        attend_back_kernel,
        [shape((t, 128), f32), shape((t, 128), f32), shape((t, 128), bf16), shape((t, d), f32)],
        idx, probs, gatt, values, values_n, ks, ks_n, qs, name="attend_back",
    )
    out = (state + b_top + b_recv[:t].astype(f32) + swap2(b_x, "xx").astype(f32)).astype(bf16)
    back = jnp.concatenate([out[:, :width], gi[:, :width], out[:, width:], gi[:, width:]], 1)
    mf = after(mf, back)
    back = from_chips(back)
    kv_recv = swap2(jnp.concatenate([vsend, ksend], 1), "xx")
    f_sum = add(f_keep, after(f_recv, qg))
    r_ffn = reduce_tensor(f_sum, rest)
    r_wo, r_wi = r_ffn[0], r_ffn[1]
    two = [shape((2, 4, 256, 256), bf16)] * 2
    g_uh = call(grad_u_kernel, two, idx, gated, hf, name="grad_u_hidden")
    g_pk = call(grad_pack_kernel, [shape((2, 4, 256, 512), bf16)] * 2, idx, mf, cat, name="grad_pack")
    gv, gs, ga, own, send = call(
        mixer_back_kernel,
        [shape((t, d), bf16), shape((t, 128), bf16), shape((8, 128), f32), shape((2, t, dh), f32), shape((2, t, dh), bf16)],
        idx, vown, kv_recv, value_pre, *wv, after(cat, g_uh[0], g_pk[0], f_sum, back), *wp, ws, qk_affine, shp, qg, kown,
        name="mixer_back", limit=56,
        scratch=[pltpu.VMEM((t, d), f32)],
    )
    both = (own + swap2(send, "core").astype(f32)).astype(bf16)
    both = jnp.concatenate([both[0, :, :width], both[1, :, :width], both[0, :, width:], both[1, :, width:]], 1)
    both = from_chips(both)
    grad_mixer, normed_part = both[:, :width], both[:, width:]
    *g_wv, gws = call(grad_value_kernel, two + [shape((d, 128), f32)], idx, nf, gv, mf, gs, name="grad_w_value")
    pair_pk = add(g_pk[0], swap2(g_pk[1], "yy"))
    pair_uh = add(g_uh[0], swap2(g_uh[1], "xx"))
    ema_grad, g_par = ema_bwd(after(grad_mixer, g_wv[0], pair_pk, pair_uh), mixed, normed, par, skip, s0)
    outputs = back[:, :width].astype(f32)
    gi_direct = back[:, width:].astype(f32)
    p_pk = add(pair_pk[0], swap2(pair_pk[1], "xx"))
    p_uh = add(pair_uh[0], swap2(pair_uh[1], "yy"))
    p_wv = reduce_plane(*g_wv, "xx", "yy", ema_grad)
    grad_normed = normed_part.astype(f32) + ema_grad
    g_norm_in = jnp.sum(grad_normed * unit_in, axis=0)
    gn = grad_normed * norm_in_own
    sums = sum_over(jnp.stack([jnp.sum(gn, 1), jnp.sum(gn * unit_in, 1)]), "tensor", 4) / d
    grad_inputs = gi_direct + inv_in * (gn - sums[0][:, None] - unit_in * sums[1][:, None])

    r_pk = reduce_tensor_direct(p_pk, rest, z)
    r_all = reduce_tensor_direct(jnp.concatenate([p_uh, p_wv], 2), rest, z)
    r_uh, r_wv = r_all[:, 0:256], r_all[:, 256:]

    wide = lax.dynamic_update_slice(jnp.zeros((d,), f32), gno[0], (c * dh,)).reshape(4, 2, 128)
    wide = jnp.concatenate([wide, jnp.stack([ga] * 4), jnp.zeros((4, 6, 128), f32), gws.reshape(4, width, 128)], 1)
    wide = lax.psum_scatter(after(wide.astype(bf16), r_wo), "tensor", scatter_dimension=0).astype(f32)
    near = ("core", "xx", "yy")
    small = jnp.concatenate([g_par, g_norm_in[None, :]], 0)
    small = sum_devices(jnp.concatenate([small[:, :128], small[:, 128:], wide], 0), rest, near)
    wide = small[146:]
    small = jnp.concatenate([small[:73], small[73:146]], 1)
    gno, gaff = wide[0:2].reshape(-1), wide[2:5]
    dp = rest * 8
    me = lax.axis_index(DPS)
    o_ws = lax.dynamic_slice_in_dim(wide[16:], me * (128 // dp), 128 // dp, 1)

    r = lax.axis_index("rest")

    def split_join(g, dim, axis):
        i = lax.axis_index(axis)
        n = g.shape[dim] // 2
        keep = lax.dynamic_slice_in_dim(g, i * n, n, dim)
        send = lax.dynamic_slice_in_dim(g, (1 - i) * n, n, dim)
        return pick(i == 0, keep, swap2(send, axis), 1 - dim)

    def finish(g, dim):
        if rest > 1:
            n = g.shape[dim] // rest
            g = lax.dynamic_slice_in_dim(g, r * n, n, dim)
        return split_join(g, dim, "core").astype(f32)
    o_wv = finish(r_wv.astype(bf16), 0)
    o_wi = finish(split_join(r_wi, 1, "xx"), 1).T
    o_wo = finish(split_join(r_wo, 1, "xx"), 1)
    o_uh = finish(r_uh.astype(bf16), 1)
    o_wr, both = r_pk[:, 0:256], r_pk[:, 256:512].astype(bf16)
    if rest > 1:
        n = o_wr.shape[1] // rest
        o_wr = lax.all_gather(o_wr, "core", axis=1, tiled=True)
        o_wr = lax.dynamic_slice_in_dim(o_wr, (r * 2 + c) * n, n, 1)
        pair = [lax.all_gather(v, ("core",) + PLANE, axis=1, tiled=True) for v in (both[:, 0:128], both[:, 128:256])]
        o_wu, o_wh = [lax.dynamic_slice_in_dim(v, me * (d // dp), d // dp, 1) for v in pair]
    else:
        both = lax.ppermute(both, PLANE + ("core",), [(b % 4 * 2 + b // 4, b) for b in range(8)])
        o_wu, o_wh = both[:, 0:128], both[:, 128:256]
    o_wr, o_wu, o_wh = o_wr.astype(f32), o_wu.astype(f32), o_wh.astype(f32)
    return (
        outputs,
        grad_inputs,
        small[72],
        o_wv,
        small[0:16].T,
        small[16:32].T,
        small[32:48].T,
        small[48:64].T,
        small[64],
        o_ws,
        gaff,
        o_wr,
        o_wu,
        o_wh,
        o_uh,
        gno,
        o_wi,
        o_wo,
    )


def solution(mesh):
    devices = np.asarray(mesh.devices)
    dp, tensor = devices.shape
    inner = Mesh(devices.reshape(2, 2, dp // 8, 2, tensor), ALL)
    t = "tensor"
    placed = (
        P(DPS, t),
        P(),
        P(None, t),
        P(t, None),
        P(t, None),
        P(t, None),
        P(t, None),
        P(t),
        P(t, None),
        P(),
        P(t, None),
        P(t, None),
        P(t, None),
        P(t, None),
        P(),
        P(None, t),
        P(t, None),
        P(DPS, t),
        P(DPS, None),
    )
    return jax.shard_map(
        on_device,
        mesh=inner,
        in_specs=placed,
        out_specs=(
            P(DPS, t),
            P(DPS, t),
            P(t),
            P(DPS, t),
            P(t, None),
            P(t, None),
            P(t, None),
            P(t, None),
            P(t),
            P(t, DPS),
            P(),
            P(t, DPS),
            P(t, DPS),
            P(t, DPS),
            P(t, DPS),
            P(t),
            P(DPS, t),
            P(t, DPS),
        ),
        check_vma=False,
    )
```
